32 devices in a mesh: lat: 4 (over x, core), lon: 8 (over z, y).
Axes of the slice: x: 2, y: 2, z: 4, core: 2. Of those that a mesh axis runs over, the one named last changes fastest.
Arguments:
- mesh_nodes: bfloat16 [8192, 512], P(('lat', 'lon')), may hold values from -6 to 6
- mesh_edges: bfloat16 [65536, 512], P(('lat', 'lon')), may hold values from -6 to 6
- grid_state: bfloat16 [128, 256, 512], P('lat', 'lon'), may hold values from -6 to 6
- decoder_edges: bfloat16 [3, 128, 256, 512], P(None, 'lat', 'lon'), may hold values from -6 to 6
- edge_send: int32 [65536], P(('lat', 'lon')), may hold values from 0 to 511
- edge_recv: int32 [65536], P(('lat', 'lon')), may hold values from -1 to 255, as said below
- halo_lists: int32 [32, 32, 8], P(('lat', 'lon')), may hold values from 0 to 255
- decoder_lists: int32 [32, 32, 4], P(('lat', 'lon')), may hold values from 0 to 255
- decoder_sources: int32 [3, 128, 256], P(None, 'lat', 'lon'), may hold values from 0 to 127
- edge_first: bfloat16 [2, 1536, 512], replicated, may hold values from -0.15625 to 0.15625
- edge_second: bfloat16 [2, 512, 512], replicated, may hold values from -0.25 to 0.25
- node_first: bfloat16 [2, 1024, 512], replicated, may hold values from -0.1875 to 0.1875
- node_second: bfloat16 [2, 512, 512], replicated, may hold values from -0.25 to 0.25
- decoder_first: bfloat16 [1536, 512], replicated, may hold values from -0.15625 to 0.15625
- decoder_second: bfloat16 [512, 512], replicated, may hold values from -0.25 to 0.25
- grid_first: bfloat16 [1024, 512], replicated, may hold values from -0.1875 to 0.1875
- grid_second: bfloat16 [512, 512], replicated, may hold values from -0.25 to 0.25
Outputs:
- mesh_final: bfloat16 [8192, 512], P(('lat', 'lon'))
- grid_final: bfloat16 [128, 256, 512], P('lat', 'lon')
The draws below stay inside these ranges and needn't reach their ends.
Inputs may be any that keep to these rules, and one draw needn't show every extreme that they name: `edge_recv`: on each partition the live edges come first; their number is a multiple of 128, at least 128 and at most 2048, and some partition has 2048; live receivers are local node rows, padding slots hold -1.
All inputs are finite; a program needn't handle non-finite values.
Results may differ from the reference program's by a relative error of at most 0.012.
Values may be sent and summed in bfloat16 or wider, within the bound.
A program may use at most 128 MiB of HBM per device.

```python
import jax
import jax.numpy as jnp
from jax import lax

W = 512
LAYERS = 2
M_DEV = 256
E_DEV = 2048
SLOTS = 8
DSLOTS = 4
TLAT = 32
TLON = 32
NODES = 8192
EDGES = 65536
LAT_ROWS = 128
LON_COLS = 256
N_LAT = 4
N_LON = 8
DEVICES = 32


def draw_edge_recv(key, part):
    block_count = E_DEV // 128
    key_blocks = jax.random.fold_in(key, 11)
    key_full = jax.random.fold_in(key, 23)
    key_rows = jax.random.fold_in(key, 37)
    raw_blocks = jax.random.randint(key_blocks, (DEVICES,), 0, block_count + 1)
    live_blocks = 1 + raw_blocks * raw_blocks // (block_count + 1)
    busiest = jax.random.randint(key_full, (), 0, DEVICES)
    live_blocks = jnp.where(jnp.arange(DEVICES) == busiest, block_count, live_blocks)
    receivers = jax.random.randint(key_rows, (DEVICES, E_DEV), 0, M_DEV)
    position = jnp.arange(E_DEV)
    chosen = jnp.where(position[None, :] < live_blocks[:, None] * 128, receivers, -1)
    return chosen.reshape(DEVICES * E_DEV).astype(jnp.int32)


def with_ends(values, stream_key, low, high):
    spot = [jax.random.randint(jax.random.fold_in(stream_key, axis), (), 0, length) for axis, length in enumerate(values.shape)]
    main_axis = values.shape.index(max(values.shape))
    next_to = spot[:main_axis] + [(spot[main_axis] + 1) % values.shape[main_axis]] + spot[main_axis + 1:]
    return values.at[tuple(spot)].set(low).at[tuple(next_to)].set(high)


def shard_levels(rng, shape, pieces, low, largest):
    loudness = 1.0
    for axis_at, shards_of in pieces:
        draws = jax.random.uniform(jax.random.fold_in(jax.random.fold_in(rng, 6), axis_at), (shards_of,), jnp.float32, low / len(pieces), largest / len(pieces))
        loudness = loudness * jnp.repeat(jnp.exp(draws), shape[axis_at] // shards_of).reshape((-1,) + (1,) * (len(shape) - 1 - axis_at))
    return loudness


def gaussian(stream_key, shape, deviation, limit, shards=(), held_as=jnp.bfloat16):
    gain = shard_levels(stream_key, shape, shards, -0.22, 0.18) if shards else 1.0
    values = jax.random.normal(stream_key, shape, jnp.float32) * deviation * gain
    return jnp.minimum(jnp.maximum(values, -limit), limit).astype(held_as)


def setup_inputs(seed: int = 0) -> dict:
    key_of = jax.random.split(jax.random.key(seed), 18)
    mesh_nodes = gaussian(key_of[0], (NODES, W), 1.0, 6.0, ((0, 32),))
    mesh_edges = gaussian(key_of[1], (EDGES, W), 1.0, 6.0, ((0, 32),))
    grid_state = gaussian(key_of[2], (LAT_ROWS, LON_COLS, W), 1.0, 6.0, ((0, 4), (1, 8)))
    decoder_edges = gaussian(key_of[3], (3, LAT_ROWS, LON_COLS, W), 1.0, 6.0, ((1, 4), (2, 8)))
    edge_send = with_ends(jax.random.randint(key_of[4], (EDGES,), 0, M_DEV + DEVICES * SLOTS), jax.random.fold_in(key_of[4], 1), 0, (M_DEV + DEVICES * SLOTS) - 1).astype(jnp.int32)
    edge_recv = draw_edge_recv(jax.random.fold_in(key_of[17], 71), 0)
    halo_lists = with_ends(jax.random.randint(key_of[6], (DEVICES, DEVICES, SLOTS), 0, M_DEV), jax.random.fold_in(key_of[6], 1), 0, M_DEV - 1).astype(jnp.int32)
    decoder_lists = with_ends(jax.random.randint(key_of[7], (DEVICES, DEVICES, DSLOTS), 0, M_DEV), jax.random.fold_in(key_of[7], 1), 0, M_DEV - 1).astype(jnp.int32)
    decoder_sources = with_ends(jax.random.randint(key_of[8], (3, LAT_ROWS, LON_COLS), 0, DEVICES * DSLOTS), jax.random.fold_in(key_of[8], 1), 0, (DEVICES * DSLOTS) - 1).astype(jnp.int32)
    edge_first = gaussian(key_of[9], (LAYERS, 3 * W, W), (3 * W) ** -0.5, 0.15625)
    edge_second = gaussian(key_of[10], (LAYERS, W, W), W ** -0.5, 0.25)
    node_first = gaussian(key_of[11], (LAYERS, 2 * W, W), (2 * W) ** -0.5, 0.1875)
    node_second = gaussian(key_of[12], (LAYERS, W, W), W ** -0.5, 0.25)
    decoder_first = gaussian(key_of[13], (3 * W, W), (3 * W) ** -0.5, 0.15625)
    decoder_second = gaussian(key_of[14], (W, W), W ** -0.5, 0.25)
    grid_first = gaussian(key_of[15], (2 * W, W), (2 * W) ** -0.5, 0.1875)
    grid_second = gaussian(key_of[16], (W, W), W ** -0.5, 0.25)
    return dict(mesh_nodes=mesh_nodes, mesh_edges=mesh_edges, grid_state=grid_state, decoder_edges=decoder_edges, edge_send=edge_send, edge_recv=edge_recv, halo_lists=halo_lists, decoder_lists=decoder_lists, decoder_sources=decoder_sources, edge_first=edge_first, edge_second=edge_second, node_first=node_first, node_second=node_second, decoder_first=decoder_first, decoder_second=decoder_second, grid_first=grid_first, grid_second=grid_second)


epsilon = 1e-05

def normalize(values):
    average = lax.optimization_barrier(jnp.mean(values, axis=-1, keepdims=True))
    centered = values - average
    spread = lax.optimization_barrier(jnp.mean(centered * centered, axis=-1, keepdims=True))
    return centered * lax.rsqrt(spread + epsilon)

def perceptron(inputs, layer_one, layer_two):
    hidden = jax.nn.silu(jnp.dot(inputs, layer_one, preferred_element_type=jnp.float32)).astype(jnp.bfloat16)
    return normalize(jnp.dot(hidden, layer_two, preferred_element_type=jnp.float32))

def mesh_layer(nodes_now, edges_now, edge_send, edge_recv, halo_lists, w_edge1, w_edge2, w_node1, w_node2):
    feature_width = nodes_now.shape[1]
    node_blocks = nodes_now.reshape(DEVICES, M_DEV, feature_width)
    edge_blocks = edges_now.reshape(DEVICES, E_DEV, feature_width)
    send_blocks = edge_send.reshape(DEVICES, E_DEV)
    recv_blocks = edge_recv.reshape(DEVICES, E_DEV)

    def one_part(device):
        own_rows = node_blocks[device]
        chosen = halo_lists[:, device, :]
        remote = jnp.take_along_axis(node_blocks, chosen[:, :, None], axis=1).reshape(DEVICES * SLOTS, feature_width)
        lookup = jnp.concatenate([own_rows, remote], axis=0)
        senders = jnp.take(lookup, send_blocks[device], axis=0)
        targets = recv_blocks[device]
        receivers = jnp.take(own_rows, jnp.maximum(targets, 0), axis=0)
        edge_rows = edge_blocks[device]
        inputs = jnp.concatenate([edge_rows, senders, receivers], axis=1)
        result = perceptron(inputs, w_edge1, w_edge2)
        message = lax.optimization_barrier(result.astype(jnp.bfloat16)).astype(jnp.float32)
        fresh = (edge_rows.astype(jnp.float32) + result).astype(jnp.bfloat16)
        segment = jnp.where(targets >= 0, targets, M_DEV).astype(jnp.int32)
        summed = jax.ops.segment_sum(message, segment, num_segments=M_DEV + 1)[:M_DEV]
        return (fresh, summed.astype(jnp.bfloat16))
    fresh_edges, gathered = lax.map(one_part, jnp.arange(DEVICES, dtype=jnp.int32))
    gathered = gathered.reshape(NODES, feature_width)
    inputs = jnp.concatenate([nodes_now, gathered], axis=1)
    result = perceptron(inputs, w_node1, w_node2)
    fresh_nodes = (nodes_now.astype(jnp.float32) + result).astype(jnp.bfloat16)
    return (fresh_nodes, fresh_edges.reshape(EDGES, feature_width))

def reference(mesh_nodes, mesh_edges, grid_state, decoder_edges, edge_send, edge_recv, halo_lists, decoder_lists, decoder_sources, edge_first, edge_second, node_first, node_second, decoder_first, decoder_second, grid_first, grid_second):
    nodes_now, edges_now = (mesh_nodes, mesh_edges)
    for layer in range(LAYERS):
        nodes_now, edges_now = mesh_layer(nodes_now, edges_now, edge_send, edge_recv, halo_lists, edge_first[layer], edge_second[layer], node_first[layer], node_second[layer])
    feature_width = nodes_now.shape[1]
    cells = TLAT * TLON
    node_blocks = nodes_now.reshape(DEVICES, M_DEV, feature_width)
    tiles = grid_state.reshape(N_LAT, TLAT, N_LON, TLON, feature_width).transpose(0, 2, 1, 3, 4).reshape(DEVICES, cells, feature_width)
    edge_tiles = decoder_edges.reshape(3, N_LAT, TLAT, N_LON, TLON, feature_width).transpose(1, 3, 0, 2, 4, 5).reshape(DEVICES, 3, cells, feature_width)
    source_tiles = decoder_sources.reshape(3, N_LAT, TLAT, N_LON, TLON).transpose(1, 3, 0, 2, 4).reshape(DEVICES, 3, cells)

    def one_tile(device):
        chosen = decoder_lists[:, device, :]
        lookup = jnp.take_along_axis(node_blocks, chosen[:, :, None], axis=1).reshape(DEVICES * DSLOTS, feature_width)
        grid_tile = tiles[device]
        summed = jnp.zeros((cells, feature_width), jnp.float32)
        for branch in range(3):
            mesh_rows = jnp.take(lookup, source_tiles[device, branch], axis=0)
            inputs = jnp.concatenate([edge_tiles[device, branch], mesh_rows, grid_tile], axis=1)
            result = perceptron(inputs, decoder_first, decoder_second)
            summed = summed + lax.optimization_barrier(result.astype(jnp.bfloat16)).astype(jnp.float32)
        gathered = summed.astype(jnp.bfloat16)
        result = perceptron(jnp.concatenate([grid_tile, gathered], axis=1), grid_first, grid_second)
        return (grid_tile.astype(jnp.float32) + result).astype(jnp.bfloat16)
    decoded = lax.map(one_tile, jnp.arange(DEVICES, dtype=jnp.int32))
    grid_final = decoded.reshape(N_LAT, N_LON, TLAT, TLON, feature_width).transpose(0, 2, 1, 3, 4).reshape(TLAT * N_LAT, TLON * N_LON, feature_width)
    return (nodes_now, grid_final)
```

```python
import functools

import jax
import jax.numpy as jnp
from jax import lax
from jax.experimental import pallas as pl
from jax.experimental.pallas import tpu as pltpu
from jax.sharding import PartitionSpec as P

EPS = 1e-05
BF = jnp.bfloat16
F32 = jnp.float32
ROWS = 256
LANES = 128


def dot(a, b):
    return jnp.dot(a, b, preferred_element_type=F32)


def silu(v):
    half = 0.5 * v
    return half + half * jnp.tanh(half)


def normalize(values):
    average = jnp.mean(values, axis=-1, keepdims=True)
    centered = values - average
    spread = jnp.mean(centered * centered, axis=-1, keepdims=True)
    return centered * lax.rsqrt(spread + EPS)


def onehot(column, codes):
    return jnp.where(column == codes, 1.0, 0.0).astype(BF)


def kernel(
    dims,
    nodes_h, edges_h, grid_h, dedges_h,
    send_r, recv_r, halo_r, dlist_r, src_r,
    ef_h, es_h, nf_h, ns_h, df_h, ds_h, gf_h, gs_h,
    mesh_o, grid_o,
    nodes, edges, grid, dedges, ef, es, nf, ns, df, ds, gf, gs,
    index_a, index_h, index_d,
    pick, pick_t, dpick, table, dtable, early, early_grid, total,
    out0, out1, out2, in0, in1, in2,
    load_sem, send_sem, recv_sem, done_sem,
):
    n_lat, n_lon = dims
    count = n_lat * n_lon
    me = lax.axis_index("lat") * n_lon + lax.axis_index("lon")
    own, width = nodes.shape
    slots = edges.shape[0]
    layers = ef.shape[0]
    halo_slots = halo_r.shape[1]
    dec_slots = dlist_r.shape[1]
    cells = grid.shape[0]
    branches = src_r.shape[0]
    tile_rows, tile_cols = src_r.shape[1], src_r.shape[2]
    table_rows = own + count * halo_slots

    loads = []

    def load(src, dst):
        copy = pltpu.make_async_copy(src, dst, load_sem.at[len(loads)])
        loads.append(copy)
        copy.start()
        return copy

    def at(q):
        return (lax.div(q, n_lon), lax.rem(q, n_lon))

    l_nodes = load(nodes_h, nodes)
    l_ef = [load(ef_h.at[0], ef.at[0])]
    l_edges = load(edges_h, edges)
    l_es = [load(es_h.at[0], es.at[0])]
    l_nf = [load(nf_h.at[0], nf.at[0])]
    l_ns = [load(ns_h.at[0], ns.at[0])]

    barrier = pltpu.get_barrier_semaphore()

    @pl.loop(1, count)
    def _(step):
        pl.semaphore_signal(
            barrier, inc=1, device_id=at(lax.rem(me + step, count)),
            device_id_type=pl.DeviceIdType.MESH,
        )

    index_a[...] = jnp.zeros_like(index_a)
    index_h[...] = jnp.zeros_like(index_h)
    index_d[...] = jnp.zeros_like(index_d)
    groups = slots // LANES
    index_a[0:groups, :] = send_r[...]
    index_a[groups : 2 * groups, :] = recv_r[...]
    for b in range(branches):
        first = 2 * groups + b * tile_rows
        index_a[first : first + tile_rows, 0:tile_cols] = src_r[b]
    index_h[0:count, 0:halo_slots] = halo_r[...]
    index_d[0:count, 0:dec_slots] = dlist_r[...]
    index_d[0:count, dec_slots : 2 * dec_slots] = dlist_r[...]
    columns_a = jnp.transpose(index_a[...])
    columns_h = jnp.transpose(index_h[...])
    columns_d = jnp.transpose(index_d[...])

    def lists_pick(columns, per):
        rows = jnp.concatenate(
            [jnp.broadcast_to(columns[0:per, q : q + 1], (per, own)) for q in range(count)], axis=0
        )
        codes = lax.broadcasted_iota(jnp.int32, (per * count, own), 1)
        return jnp.where(rows == codes, 1.0, 0.0).astype(BF)

    halo_pick = lists_pick(columns_h, halo_slots)

    def post(outgoing, incoming, which):
        @pl.loop(1, count)
        def _(step):
            q = lax.rem(me + step, count)
            pltpu.make_async_remote_copy(
                src_ref=outgoing.at[q],
                dst_ref=incoming.at[me],
                send_sem=send_sem.at[which],
                recv_sem=recv_sem.at[which],
                device_id=at(q),
                device_id_type=pl.DeviceIdType.MESH,
            ).start()

        incoming[pl.ds(me, 1)] = outgoing[pl.ds(me, 1)]

    def drain(buffer, sem):
        whole = buffer.at[pl.ds(0, count - 1)]
        pltpu.make_async_copy(whole, whole, sem).wait()

    def halo_send(outgoing, incoming, which):
        chosen = dot(halo_pick, nodes[...])
        outgoing[...] = chosen.reshape(count, halo_slots, width).astype(BF)
        if which == 0:
            pl.semaphore_wait(barrier, count - 1)
        post(outgoing, incoming, which)

    l_nodes.wait()
    halo_send(out0, in0, 0)

    l_ef += [load(ef_h.at[l], ef.at[l]) for l in range(1, layers)]
    l_es += [load(es_h.at[l], es.at[l]) for l in range(1, layers)]
    l_nf += [load(nf_h.at[l], nf.at[l]) for l in range(1, layers)]
    l_ns += [load(ns_h.at[l], ns.at[l]) for l in range(1, layers)]
    l_df = load(df_h, df)
    l_grid = load(grid_h, grid)
    l_dedges = load(dedges_h, dedges)
    l_gf = load(gf_h, gf)
    l_ds = load(ds_h, ds)
    l_gs = load(gs_h, gs)

    def rows_of(step):
        return pl.ds(pl.multiple_of(step * ROWS, ROWS), ROWS)

    send_codes = lax.broadcasted_iota(jnp.int32, (LANES, table_rows), 1)
    recv_codes = lax.broadcasted_iota(jnp.int32, (LANES, own), 1)
    node_codes = lax.broadcasted_iota(jnp.int32, (own, LANES), 0)
    for g in range(groups):
        span = slice(g * LANES, (g + 1) * LANES)
        pick[span, 0:table_rows] = onehot(columns_a[:, g : g + 1], send_codes)
        pick[span, table_rows:] = onehot(columns_a[:, groups + g : groups + g + 1], recv_codes)
        pick_t[:, span] = jnp.where(recv_r[g : g + 1, :] == node_codes, 1.0, 0.0).astype(BF)

    outs, ins = [out0, out1], [in0, in1]
    for l in range(layers):
        l_ef[l].wait()
        if l == 0:
            l_edges.wait()
        table[0:own, :] = dot(nodes[...], ef[l, width : 2 * width, :]).astype(BF)
        table[table_rows:, :] = dot(nodes[...], ef[l, 2 * width :, :]).astype(BF)

        @pl.loop(0, slots // ROWS)
        def _(step):
            rows = rows_of(step)
            early[rows, :] = dot(edges[rows, :], ef[l, 0:width, :])

        if l == 1 or layers == 1:
            point_codes = lax.broadcasted_iota(jnp.int32, (tile_cols, 2 * dec_slots * count), 1)
            point_codes = (point_codes // (2 * dec_slots)) * dec_slots + point_codes % dec_slots
            for b in range(branches):
                for r in range(tile_rows):
                    lane = 2 * groups + b * tile_rows + r
                    first = b * cells + r * tile_cols
                    dpick[first : first + tile_cols, :] = onehot(
                        columns_a[0:tile_cols, lane : lane + 1], point_codes
                    )

        drain(ins[l], recv_sem.at[l])
        far = ins[l][...].astype(F32).reshape(count * halo_slots, width).astype(BF)
        table[own:table_rows, :] = dot(far, ef[l, width : 2 * width, :]).astype(BF)
        total[...] = jnp.zeros_like(total)
        l_es[l].wait()

        @pl.loop(0, slots // ROWS)
        def _(step):
            rows = rows_of(step)
            hidden = silu(early[rows, :] + dot(pick[rows, :], table[...])).astype(BF)
            result = normalize(dot(hidden, es[l]))
            total[...] += dot(pick_t[:, rows], result.astype(BF))
            if l < layers - 1:
                edges[rows, :] = (edges[rows, :].astype(F32) + result).astype(BF)

        l_nf[l].wait()
        l_ns[l].wait()
        hidden = silu(
            dot(nodes[...], nf[l, 0:width, :]) + dot(total[...].astype(BF), nf[l, width:, :])
        ).astype(BF)
        result = normalize(dot(hidden, ns[l]))
        nodes[...] = (nodes[...].astype(F32) + result).astype(BF)
        if l < layers - 1:
            halo_send(outs[l + 1], ins[l + 1], l + 1)

    half = width // 2
    chosen = dot(lists_pick(columns_d, 2 * dec_slots), nodes[...])
    place = lax.broadcasted_iota(jnp.int32, (2 * dec_slots * count, half), 0)
    upper = (place % (2 * dec_slots)) >= dec_slots
    chosen = jnp.where(upper, chosen[:, half:], chosen[:, :half])
    out2[...] = chosen.reshape(count, 2 * dec_slots, half).astype(BF)
    post(out2, in2, layers)
    mesh_copy = pltpu.make_async_copy(nodes, mesh_o, done_sem.at[0])
    mesh_copy.start()

    l_df.wait()
    l_grid.wait()
    l_dedges.wait()
    l_gf.wait()
    steps = cells // ROWS

    @pl.loop(0, steps)
    def _(step):
        rows = rows_of(step)
        here = grid[rows, :]
        shared = dot(here, df[2 * width :, :])
        for b in range(branches):
            span = pl.ds(pl.multiple_of(b * cells + step * ROWS, ROWS), ROWS)
            early[span, :] = shared + dot(dedges[span, :], df[0:width, :])
        early_grid[rows, :] = dot(here, gf[0:width, :])

    l_ds.wait()
    l_gs.wait()
    drain(in2, recv_sem.at[layers])
    far = in2[...].astype(F32).reshape(count * 2 * dec_slots, half).astype(BF)
    place = lax.broadcasted_iota(jnp.int32, (2 * dec_slots * count, width), 0)
    upper = (place % (2 * dec_slots)) >= dec_slots
    dtable[...] = jnp.where(
        upper, dot(far, df[width + half : 2 * width, :]), dot(far, df[width : width + half, :])
    ).astype(BF)

    @pl.loop(0, steps)
    def _(step):
        rows = rows_of(step)
        summed = None
        for b in range(branches):
            span = pl.ds(pl.multiple_of(b * cells + step * ROWS, ROWS), ROWS)
            hidden = silu(early[span, :] + dot(dpick[span, :], dtable[...])).astype(BF)
            result = normalize(dot(hidden, ds[...])).astype(BF).astype(F32)
            summed = result if summed is None else summed + result
        hidden = silu(early_grid[rows, :] + dot(summed.astype(BF), gf[width:, :])).astype(BF)
        result = normalize(dot(hidden, gs[...]))
        grid[rows, :] = (grid[rows, :].astype(F32) + result).astype(BF)
        pltpu.make_async_copy(grid.at[rows], grid_o.at[rows], done_sem.at[1 + step]).start()

    for b, buffer in enumerate([out0, out1, out2]):
        drain(buffer, send_sem.at[b])
    mesh_copy.wait()

    @pl.loop(0, steps)
    def _(step):
        rows = rows_of(step)
        pltpu.make_async_copy(grid.at[rows], grid_o.at[rows], done_sem.at[1 + step]).wait()


def shards(
    dims,
    mesh_nodes, mesh_edges, grid_state, decoder_edges, edge_send, edge_recv, halo_lists,
    decoder_lists, decoder_sources, edge_first, edge_second, node_first, node_second,
    decoder_first, decoder_second, grid_first, grid_second,
):
    own, width = mesh_nodes.shape
    slots = mesh_edges.shape[0]
    tile_lat, tile_lon = grid_state.shape[0], grid_state.shape[1]
    cells = tile_lat * tile_lon
    branches = decoder_edges.shape[0]
    count, halo_slots = halo_lists.shape[1], halo_lists.shape[2]
    dec_slots = decoder_lists.shape[2]
    layers = edge_first.shape[0]
    table_rows = own + count * halo_slots
    list_rows = -(-count // LANES) * LANES
    index_rows = -(-(2 * slots // LANES + branches * tile_lat) // LANES) * LANES
    hbm = pl.BlockSpec(memory_space=pl.ANY)
    vmem = pl.BlockSpec(memory_space=pltpu.VMEM)

    big = [mesh_nodes, mesh_edges, grid_state.reshape(cells, width),
           decoder_edges.reshape(branches * cells, width)]
    weights = [edge_first, edge_second, node_first, node_second,
               decoder_first, decoder_second, grid_first, grid_second]
    small = [edge_send.reshape(-1, LANES), edge_recv.reshape(-1, LANES), halo_lists[0],
             decoder_lists[0], decoder_sources]

    held = [pltpu.VMEM(a.shape, a.dtype) for a in big + weights]
    scratch = held + [
        pltpu.VMEM((index_rows, LANES), jnp.int32),
        pltpu.VMEM((list_rows, LANES), jnp.int32),
        pltpu.VMEM((list_rows, LANES), jnp.int32),
        pltpu.VMEM((slots, table_rows + own), BF),
        pltpu.VMEM((own, slots), BF),
        pltpu.VMEM((branches * cells, 2 * dec_slots * count), BF),
        pltpu.VMEM((table_rows + own, width), BF),
        pltpu.VMEM((2 * dec_slots * count, width), BF),
        pltpu.VMEM((max(slots, branches * cells), width), F32),
        pltpu.VMEM((cells, width), F32),
        pltpu.VMEM((own, width), F32),
        pltpu.VMEM((count, halo_slots, width), BF),
        pltpu.VMEM((count, halo_slots, width), BF),
        pltpu.VMEM((count, 2 * dec_slots, width // 2), BF),
        pltpu.VMEM((count, halo_slots, width), BF),
        pltpu.VMEM((count, halo_slots, width), BF),
        pltpu.VMEM((count, 2 * dec_slots, width // 2), BF),
        pltpu.SemaphoreType.DMA((8 + 4 * layers,)),
        pltpu.SemaphoreType.DMA((layers + 1,)),
        pltpu.SemaphoreType.DMA((layers + 1,)),
        pltpu.SemaphoreType.DMA((1 + cells // ROWS,)),
    ]
    mesh_final, grid_final = pl.pallas_call(
        functools.partial(kernel, dims),
        out_shape=(
            jax.ShapeDtypeStruct((own, width), BF),
            jax.ShapeDtypeStruct((cells, width), BF),
        ),
        in_specs=[hbm] * len(big) + [vmem] * len(small) + [hbm] * len(weights),
        out_specs=(hbm, hbm),
        scratch_shapes=scratch,
        compiler_params=pltpu.CompilerParams(
            collective_id=0, has_side_effects=True, vmem_limit_bytes=60 * 1024 * 1024
        ),
        name="processor",
    )(*big, *small, *weights)
    return mesh_final, grid_final.reshape(tile_lat, tile_lon, width)


def solution(mesh):
    both = ("lat", "lon")
    placed = (
        P(both, None),
        P(both, None),
        P("lat", "lon", None),
        P(None, "lat", "lon", None),
        P(both),
        P(both),
        P(both, None, None),
        P(both, None, None),
        P(None, "lat", "lon"),
    ) + (P(),) * 8
    dims = (mesh.shape["lat"], mesh.shape["lon"])
    return jax.shard_map(
        functools.partial(shards, dims),
        mesh=mesh,
        in_specs=placed,
        out_specs=(P(both, None), P("lat", "lon", None)),
        check_vma=False,
    )
```

```python
import functools

import jax
import jax.numpy as jnp
from jax import lax
from jax.experimental import pallas as pl
from jax.experimental.pallas import tpu as pltpu
from jax.sharding import PartitionSpec as P

EPS = 1e-05
BF = jnp.bfloat16
F32 = jnp.float32
ROWS = 256
LANES = 128


def dot(a, b):
    return jnp.dot(a, b, preferred_element_type=F32)


def silu(half):
    half = half.astype(BF)
    return half + half * jnp.tanh(half)


def normalize(centered):
    spread = jnp.mean(centered * centered, axis=-1, keepdims=True)
    return centered * lax.rsqrt(spread + EPS)


def center(ref):
    values = ref[...].astype(F32)
    ref[...] = (values - jnp.mean(values, axis=-1, keepdims=True)).astype(BF)


def onehot(indices, codes):
    return jnp.where(indices == codes, BF(1), BF(0))


def lane_codes(rows):
    return lax.broadcasted_iota(jnp.int32, (rows, LANES), 1)


def fill(ref, rows, first, columns, codes, blocks, base):
    shape = codes.shape
    wide = [jnp.broadcast_to(column, shape) for column in columns]
    for k in range(blocks):
        low = first + k * LANES
        j = base * k // 256
        near = codes + BF(base * k - 256 * j)
        ref[rows, low : low + LANES] = onehot(wide[j], near)


def kernel(
    dims,
    nodes_h, edges_h, grid_h, dedges_h,
    send_r, recv_r, halo_r, dlist_r, src_r,
    ef_h, es_h, nf_h, ns_h, df_h, ds_h, gf_h, gs_h,
    mesh_o, grid_o,
    nodes, edges, grid, dedges, ef, es, nf, ns, df, ds, gf, gs,
    index_a, index_d,
    pick, pick_t, dpick, table, dtable, early, early_grid, total,
    out0, out1, out2, in0, in1, in2,
    load_sem, send_sem, recv_sem, done_sem,
):
    n_lat, n_lon = dims
    count = n_lat * n_lon
    me = lax.axis_index("lat") * n_lon + lax.axis_index("lon")
    own, width = nodes.shape
    slots = edges.shape[0]
    layers = ef.shape[0]
    halo_slots = halo_r.shape[0]
    dec_slots = dlist_r.shape[0]
    cells = grid.shape[0]
    branches = src_r.shape[0]
    tile_rows, tile_cols = src_r.shape[1], src_r.shape[2]
    table_rows = own + count * halo_slots

    loads = []

    def load(src, dst):
        copy = pltpu.make_async_copy(src, dst, load_sem.at[len(loads)])
        loads.append(copy)
        copy.start()
        return copy

    def at(q):
        return (lax.div(q, n_lon), lax.rem(q, n_lon))

    l_nodes = load(nodes_h, nodes)
    l_ef = [load(ef_h.at[0], ef.at[0])]
    l_edges = load(edges_h, edges)
    l_es = [load(es_h.at[0], es.at[0])]
    l_nf = [load(nf_h.at[0], nf.at[0])]
    l_ns = [load(ns_h.at[0], ns.at[0])]

    barrier = pltpu.get_barrier_semaphore()

    @pl.loop(1, count)
    def _(step):
        pl.semaphore_signal(
            barrier, inc=1, device_id=at(lax.rem(me + step, count)),
            device_id_type=pl.DeviceIdType.MESH,
        )

    index_a[...] = jnp.zeros_like(index_a)
    groups = slots // LANES
    index_a[0:groups, :] = send_r[...]
    index_a[groups : 2 * groups, :] = recv_r[...]
    for b in range(branches):
        first = 2 * groups + b * tile_rows
        index_a[first : first + tile_rows, 0:tile_cols] = src_r[b]
    index_d[0:dec_slots, :] = dlist_r[...]
    index_d[dec_slots : 2 * dec_slots, :] = dlist_r[...]

    def lists_pick(columns, per):
        rows = jnp.concatenate(
            [jnp.broadcast_to(columns[0:per, q : q + 1], (per, own)) for q in range(count)], axis=0
        )
        codes = lax.broadcasted_iota(jnp.int32, (per * count, own), 1)
        return jnp.where(rows == codes, 1.0, 0.0).astype(BF)

    halo_pick = lists_pick(halo_r[...], halo_slots)

    def post(outgoing, incoming, which):
        @pl.loop(1, count)
        def _(step):
            q = lax.rem(me + step, count)
            pltpu.make_async_remote_copy(
                src_ref=outgoing.at[q],
                dst_ref=incoming.at[me],
                send_sem=send_sem.at[which],
                recv_sem=recv_sem.at[which],
                device_id=at(q),
                device_id_type=pl.DeviceIdType.MESH,
            ).start()

        incoming[pl.ds(me, 1)] = outgoing[pl.ds(me, 1)]

    def drain(buffer, sem):
        whole = buffer.at[pl.ds(0, count - 1)]
        pltpu.make_async_copy(whole, whole, sem).wait()

    def halo_send(outgoing, incoming, which):
        chosen = dot(halo_pick, nodes[...])
        outgoing[...] = chosen.reshape(count, halo_slots, width).astype(BF)
        if which == 0:
            pl.semaphore_wait(barrier, count - 1)
        post(outgoing, incoming, which)

    l_nodes.wait()
    halo_send(out0, in0, 0)

    l_ef += [load(ef_h.at[l], ef.at[l]) for l in range(1, layers)]
    l_es += [load(es_h.at[l], es.at[l]) for l in range(1, layers)]
    l_nf += [load(nf_h.at[l], nf.at[l]) for l in range(1, layers)]
    l_ns += [load(ns_h.at[l], ns.at[l]) for l in range(1, layers)]
    l_df = load(df_h, df)
    l_grid = load(grid_h, grid)
    l_dedges = load(dedges_h, dedges)
    l_gf = load(gf_h, gf)
    l_ds = load(ds_h, ds)
    l_gs = load(gs_h, gs)

    def rows_of(step):
        return pl.ds(pl.multiple_of(step * ROWS, ROWS), ROWS)

    columns_a = jnp.transpose(index_a[...]).astype(F32)
    shifted = [(columns_a - 256.0 * j).astype(BF) for j in range(-(-table_rows // 256))]
    row_codes = lane_codes(LANES).astype(F32).astype(BF)
    node_codes = lax.broadcasted_iota(jnp.int32, (own, LANES), 0).astype(F32).astype(BF)
    for g in range(groups):
        span = slice(g * LANES, (g + 1) * LANES)
        lane, other = slice(g, g + 1), slice(groups + g, groups + g + 1)
        fill(pick, span, 0, [c[:, lane] for c in shifted], row_codes, table_rows // LANES, LANES)
        fill(pick, span, table_rows, [c[:, other] for c in shifted[: -(-own // 256)]],
             row_codes, own // LANES, LANES)
        targets = jnp.broadcast_to(recv_r[g : g + 1, :].astype(F32).astype(BF), (own, LANES))
        pick_t[:, span] = onehot(targets, node_codes)

    outs, ins = [out0, out1], [in0, in1]
    for l in range(layers):
        l_ef[l].wait()
        if l == 0:
            l_edges.wait()
        table[0:own, :] = (0.5 * dot(nodes[...], ef[l, width : 2 * width, :])).astype(BF)
        table[table_rows:, :] = (0.5 * dot(nodes[...], ef[l, 2 * width :, :])).astype(BF)

        @pl.loop(0, slots // ROWS)
        def _(step):
            rows = rows_of(step)
            early[rows, :] = 0.5 * dot(edges[rows, :], ef[l, 0:width, :])

        l_nf[l].wait()
        early_grid[0:own, :] = 0.5 * dot(nodes[...], nf[l, 0:width, :])
        l_es[l].wait()
        l_ns[l].wait()
        center(es.at[l])
        center(ns.at[l])

        if l == 1 or layers == 1:
            l_ds.wait()
            l_gs.wait()
            l_gf.wait()
            center(ds)
            center(gs)
            gf[width:, :] = gf[width:, :] * BF(0.5)
            codes = lane_codes(tile_cols)
            codes = (codes // (2 * dec_slots)) * dec_slots + codes % dec_slots
            codes = codes.astype(F32).astype(BF)
            needed = -(-dec_slots * count // 256)
            for b in range(branches):
                for r in range(tile_rows):
                    lane = 2 * groups + b * tile_rows + r
                    first = b * cells + r * tile_cols
                    fill(dpick, slice(first, first + tile_cols), 0,
                         [c[0:tile_cols, lane : lane + 1] for c in shifted[:needed]],
                         codes, 2 * dec_slots * count // LANES, LANES // 2)

        drain(ins[l], recv_sem.at[l])
        far = ins[l][...].astype(F32).reshape(count * halo_slots, width).astype(BF)
        table[own:table_rows, :] = (0.5 * dot(far, ef[l, width : 2 * width, :])).astype(BF)
        total[...] = jnp.zeros_like(total)

        @pl.loop(0, slots // ROWS)
        def _(step):
            rows = rows_of(step)
            hidden = silu(early[rows, :] + dot(pick[rows, :], table[...]))
            result = normalize(dot(hidden, es[l]))
            total[...] += dot(pick_t[:, rows], result.astype(BF))
            if l < layers - 1:
                edges[rows, :] = (edges[rows, :].astype(F32) + result).astype(BF)

        hidden = silu(
            early_grid[0:own, :] + 0.5 * dot(total[...].astype(BF), nf[l, width:, :])
        )
        result = normalize(dot(hidden, ns[l]))
        nodes[...] = (nodes[...].astype(F32) + result).astype(BF)
        if l < layers - 1:
            halo_send(outs[l + 1], ins[l + 1], l + 1)

    half = width // 2
    chosen = dot(lists_pick(index_d[...], 2 * dec_slots), nodes[...])
    place = lax.broadcasted_iota(jnp.int32, (2 * dec_slots * count, half), 0)
    upper = (place % (2 * dec_slots)) >= dec_slots
    chosen = jnp.where(upper, chosen[:, half:], chosen[:, :half])
    out2[...] = chosen.reshape(count, 2 * dec_slots, half).astype(BF)
    post(out2, in2, layers)
    mesh_copy = pltpu.make_async_copy(nodes, mesh_o, done_sem.at[0])
    mesh_copy.start()

    l_df.wait()
    l_grid.wait()
    l_dedges.wait()
    steps = cells // ROWS

    @pl.loop(0, steps)
    def _(step):
        rows = rows_of(step)
        here = grid[rows, :]
        shared = 0.5 * dot(here, df[2 * width :, :])
        for b in range(branches):
            span = pl.ds(pl.multiple_of(b * cells + step * ROWS, ROWS), ROWS)
            early[span, :] = shared + 0.5 * dot(dedges[span, :], df[0:width, :])
        early_grid[rows, :] = 0.5 * dot(here, gf[0:width, :])

    drain(in2, recv_sem.at[layers])
    far = in2[...].astype(F32).reshape(count * 2 * dec_slots, half).astype(BF)
    place = lax.broadcasted_iota(jnp.int32, (2 * dec_slots * count, width), 0)
    upper = (place % (2 * dec_slots)) >= dec_slots
    chosen = jnp.where(
        upper, dot(far, df[width + half : 2 * width, :]), dot(far, df[width : width + half, :])
    )
    dtable[...] = (0.5 * chosen).astype(BF)

    @pl.loop(0, steps)
    def _(step):
        rows = rows_of(step)
        summed = None
        for b in range(branches):
            span = pl.ds(pl.multiple_of(b * cells + step * ROWS, ROWS), ROWS)
            hidden = silu(early[span, :] + dot(dpick[span, :], dtable[...]))
            result = normalize(dot(hidden, ds[...])).astype(BF).astype(F32)
            summed = result if summed is None else summed + result
        hidden = silu(early_grid[rows, :] + dot(summed.astype(BF), gf[width:, :]))
        result = normalize(dot(hidden, gs[...]))
        grid[rows, :] = (grid[rows, :].astype(F32) + result).astype(BF)
        pltpu.make_async_copy(grid.at[rows], grid_o.at[rows], done_sem.at[1 + step]).start()

    for b, buffer in enumerate([out0, out1, out2]):
        drain(buffer, send_sem.at[b])
    mesh_copy.wait()

    @pl.loop(0, steps)
    def _(step):
        rows = rows_of(step)
        pltpu.make_async_copy(grid.at[rows], grid_o.at[rows], done_sem.at[1 + step]).wait()


def shards(
    dims,
    mesh_nodes, mesh_edges, grid_state, decoder_edges, edge_send, edge_recv, halo_lists,
    decoder_lists, decoder_sources, edge_first, edge_second, node_first, node_second,
    decoder_first, decoder_second, grid_first, grid_second,
):
    own, width = mesh_nodes.shape
    slots = mesh_edges.shape[0]
    tile_lat, tile_lon = grid_state.shape[0], grid_state.shape[1]
    cells = tile_lat * tile_lon
    branches = decoder_edges.shape[0]
    count, halo_slots = halo_lists.shape[1], halo_lists.shape[2]
    dec_slots = decoder_lists.shape[2]
    layers = edge_first.shape[0]
    table_rows = own + count * halo_slots
    index_rows = -(-(2 * slots // LANES + branches * tile_lat) // LANES) * LANES
    hbm = pl.BlockSpec(memory_space=pl.ANY)
    vmem = pl.BlockSpec(memory_space=pltpu.VMEM)

    big = [mesh_nodes, mesh_edges, grid_state.reshape(cells, width),
           decoder_edges.reshape(branches * cells, width)]
    weights = [edge_first, edge_second, node_first, node_second,
               decoder_first, decoder_second, grid_first, grid_second]
    small = [edge_send.reshape(-1, LANES), edge_recv.reshape(-1, LANES), halo_lists[0].T,
             decoder_lists[0].T, decoder_sources]

    held = [pltpu.VMEM(a.shape, a.dtype) for a in big + weights]
    scratch = held + [
        pltpu.VMEM((index_rows, LANES), jnp.int32),
        pltpu.VMEM((2 * dec_slots, count), jnp.int32),
        pltpu.VMEM((slots, table_rows + own), BF),
        pltpu.VMEM((own, slots), BF),
        pltpu.VMEM((branches * cells, 2 * dec_slots * count), BF),
        pltpu.VMEM((table_rows + own, width), BF),
        pltpu.VMEM((2 * dec_slots * count, width), BF),
        pltpu.VMEM((max(slots, branches * cells), width), F32),
        pltpu.VMEM((max(cells, own), width), F32),
        pltpu.VMEM((own, width), F32),
        pltpu.VMEM((count, halo_slots, width), BF),
        pltpu.VMEM((count, halo_slots, width), BF),
        pltpu.VMEM((count, 2 * dec_slots, width // 2), BF),
        pltpu.VMEM((count, halo_slots, width), BF),
        pltpu.VMEM((count, halo_slots, width), BF),
        pltpu.VMEM((count, 2 * dec_slots, width // 2), BF),
        pltpu.SemaphoreType.DMA((8 + 4 * layers,)),
        pltpu.SemaphoreType.DMA((layers + 1,)),
        pltpu.SemaphoreType.DMA((layers + 1,)),
        pltpu.SemaphoreType.DMA((1 + cells // ROWS,)),
    ]
    mesh_final, grid_final = pl.pallas_call(
        functools.partial(kernel, dims),
        out_shape=(
            jax.ShapeDtypeStruct((own, width), BF),
            jax.ShapeDtypeStruct((cells, width), BF),
        ),
        in_specs=[hbm] * len(big) + [vmem] * len(small) + [hbm] * len(weights),
        out_specs=(hbm, hbm),
        scratch_shapes=scratch,
        compiler_params=pltpu.CompilerParams(
            collective_id=0, has_side_effects=True, vmem_limit_bytes=60 * 1024 * 1024
        ),
        name="processor",
    )(*big, *small, *weights)
    return mesh_final, grid_final.reshape(tile_lat, tile_lon, width)


def solution(mesh):
    both = ("lat", "lon")
    placed = (
        P(both, None),
        P(both, None),
        P("lat", "lon", None),
        P(None, "lat", "lon", None),
        P(both),
        P(both),
        P(both, None, None),
        P(both, None, None),
        P(None, "lat", "lon"),
    ) + (P(),) * 8
    dims = (mesh.shape["lat"], mesh.shape["lon"])
    return jax.shard_map(
        functools.partial(shards, dims),
        mesh=mesh,
        in_specs=placed,
        out_specs=(P(both, None), P("lat", "lon", None)),
        check_vma=False,
    )
```

```python
import functools

import jax
import jax.numpy as jnp
from jax import lax
from jax.experimental import pallas as pl
from jax.experimental.pallas import tpu as pltpu
from jax.sharding import PartitionSpec as P

EPS = 1e-05
BF = jnp.bfloat16
F32 = jnp.float32
ROWS = 512
EDGE_ROWS = 512
LANES = 128


def dot(a, b):
    return jnp.dot(a, b, preferred_element_type=F32)


def silu(half):
    half = half.astype(BF)
    return half + half * jnp.tanh(half)


def normalize(centered):
    spread = jnp.mean(centered * centered, axis=-1, keepdims=True)
    return centered * lax.rsqrt(spread + EPS)


def center(ref):
    values = ref[...].astype(F32)
    ref[...] = (values - jnp.mean(values, axis=-1, keepdims=True)).astype(BF)


def onehot(indices, codes):
    return jnp.where(indices == codes, BF(1), BF(0))


def lane_codes(rows):
    return lax.broadcasted_iota(jnp.int32, (rows, LANES), 1)


def fill(ref, rows, first, columns, codes, blocks, base):
    shape = codes.shape
    wide = [jnp.broadcast_to(column, shape) for column in columns]
    for k in range(blocks):
        low = first + k * LANES
        j = base * k // 256
        near = codes + BF(base * k - 256 * j)
        ref[rows, low : low + LANES] = onehot(wide[j], near)


def kernel(
    dims,
    nodes_h, edges_h, grid_h, dedges_h,
    send_r, recv_r, halo_r, dlist_r, src_r,
    ef_h, es_h, nf_h, ns_h, df_h, ds_h, gf_h, gs_h,
    mesh_o, grid_o,
    nodes, edges, grid, dedges, ef, es, nf, ns, df, ds, gf, gs,
    index_a, index_d,
    pick, pick_t, dpick, table, dtable, early, early_grid, total,
    out0, out1, out2, in0, in1, in2,
    load_sem, send_sem, recv_sem, done_sem,
):
    n_lat, n_lon = dims
    count = n_lat * n_lon
    me = lax.axis_index("lat") * n_lon + lax.axis_index("lon")
    own, width = nodes.shape
    slots = edges.shape[0]
    layers = ef.shape[0]
    halo_slots = halo_r.shape[0]
    dec_slots = dlist_r.shape[0]
    cells = grid.shape[0]
    branches = src_r.shape[0]
    tile_rows, tile_cols = src_r.shape[1], src_r.shape[2]
    table_rows = own + count * halo_slots

    loads = []

    def load(src, dst):
        copy = pltpu.make_async_copy(src, dst, load_sem.at[len(loads)])
        loads.append(copy)
        copy.start()
        return copy

    def at(q):
        return (lax.div(q, n_lon), lax.rem(q, n_lon))

    l_nodes = load(nodes_h, nodes)
    l_ef = [load(ef_h.at[0], ef.at[0])]
    l_edges = load(edges_h, edges)
    l_es = [load(es_h.at[0], es.at[0])]
    l_nf = [load(nf_h.at[0], nf.at[0])]
    l_ns = [load(ns_h.at[0], ns.at[0])]

    barrier = pltpu.get_barrier_semaphore()

    @pl.loop(1, count)
    def _(step):
        pl.semaphore_signal(
            barrier, inc=1, device_id=at(lax.rem(me + step, count)),
            device_id_type=pl.DeviceIdType.MESH,
        )

    index_a[...] = jnp.zeros_like(index_a)
    groups = slots // LANES
    index_a[0:groups, :] = send_r[...]
    index_a[groups : 2 * groups, :] = recv_r[...]
    for b in range(branches):
        first = 2 * groups + b * tile_rows
        index_a[first : first + tile_rows, 0:tile_cols] = src_r[b]
    index_d[0:dec_slots, :] = dlist_r[...]
    index_d[dec_slots : 2 * dec_slots, :] = dlist_r[...]

    def lists_pick(columns, per):
        rows = jnp.concatenate(
            [jnp.broadcast_to(columns[0:per, q : q + 1], (per, own)) for q in range(count)], axis=0
        )
        codes = lax.broadcasted_iota(jnp.int32, (per * count, own), 1)
        return jnp.where(rows == codes, 1.0, 0.0).astype(BF)

    halo_pick = lists_pick(halo_r[...], halo_slots)

    def post(outgoing, incoming, which):
        @pl.loop(1, count)
        def _(step):
            q = lax.rem(me + step, count)
            pltpu.make_async_remote_copy(
                src_ref=outgoing.at[q],
                dst_ref=incoming.at[me],
                send_sem=send_sem.at[which],
                recv_sem=recv_sem.at[which],
                device_id=at(q),
                device_id_type=pl.DeviceIdType.MESH,
            ).start()

        incoming[pl.ds(me, 1)] = outgoing[pl.ds(me, 1)]

    def drain(buffer, sem):
        whole = buffer.at[pl.ds(0, count - 1)]
        pltpu.make_async_copy(whole, whole, sem).wait()

    def halo_send(outgoing, incoming, which):
        chosen = dot(halo_pick, nodes[...])
        outgoing[...] = chosen.reshape(count, halo_slots, width).astype(BF)
        if which == 0:
            pl.semaphore_wait(barrier, count - 1)
        post(outgoing, incoming, which)

    l_nodes.wait()
    halo_send(out0, in0, 0)

    l_ef += [load(ef_h.at[l], ef.at[l]) for l in range(1, layers)]
    l_es += [load(es_h.at[l], es.at[l]) for l in range(1, layers)]
    l_nf += [load(nf_h.at[l], nf.at[l]) for l in range(1, layers)]
    l_ns += [load(ns_h.at[l], ns.at[l]) for l in range(1, layers)]
    l_df = load(df_h, df)
    l_grid = load(grid_h, grid)
    l_dedges = load(dedges_h, dedges)
    l_gf = load(gf_h, gf)
    l_ds = load(ds_h, ds)
    l_gs = load(gs_h, gs)

    def rows_of(step, size=ROWS):
        return pl.ds(pl.multiple_of(step * size, size), size)

    columns_a = jnp.transpose(index_a[...]).astype(F32)
    shifted = [(columns_a - 256.0 * j).astype(BF) for j in range(-(-table_rows // 256))]
    row_codes = lane_codes(LANES).astype(F32).astype(BF)
    node_codes = lax.broadcasted_iota(jnp.int32, (own, LANES), 0).astype(F32).astype(BF)
    for g in range(groups):
        span = slice(g * LANES, (g + 1) * LANES)
        lane, other = slice(g, g + 1), slice(groups + g, groups + g + 1)
        fill(pick, span, 0, [c[:, lane] for c in shifted], row_codes, table_rows // LANES, LANES)
        fill(pick, span, table_rows, [c[:, other] for c in shifted[: -(-own // 256)]],
             row_codes, own // LANES, LANES)
        targets = jnp.broadcast_to(recv_r[g : g + 1, :].astype(F32).astype(BF), (own, LANES))
        pick_t[:, span] = onehot(targets, node_codes)

    outs, ins = [out0, out1], [in0, in1]
    for l in range(layers):
        l_ef[l].wait()
        if l == 0:
            l_edges.wait()
        table[0:own, :] = (0.5 * dot(nodes[...], ef[l, width : 2 * width, :])).astype(BF)
        table[table_rows:, :] = (0.5 * dot(nodes[...], ef[l, 2 * width :, :])).astype(BF)

        @pl.loop(0, slots // EDGE_ROWS)
        def _(step):
            rows = rows_of(step, EDGE_ROWS)
            early[rows, :] = 0.5 * dot(edges[rows, :], ef[l, 0:width, :])

        l_nf[l].wait()
        early_grid[0:own, :] = 0.5 * dot(nodes[...], nf[l, 0:width, :])
        l_es[l].wait()
        l_ns[l].wait()
        center(es.at[l])
        center(ns.at[l])

        if l == 1 or layers == 1:
            l_ds.wait()
            l_gs.wait()
            l_gf.wait()
            center(ds)
            center(gs)
            gf[width:, :] = gf[width:, :] * BF(0.5)
            codes = lane_codes(tile_cols)
            codes = (codes // (2 * dec_slots)) * dec_slots + codes % dec_slots
            codes = codes.astype(F32).astype(BF)
            needed = -(-dec_slots * count // 256)
            for b in range(branches):
                for r in range(tile_rows):
                    lane = 2 * groups + b * tile_rows + r
                    first = b * cells + r * tile_cols
                    fill(dpick, slice(first, first + tile_cols), 0,
                         [c[0:tile_cols, lane : lane + 1] for c in shifted[:needed]],
                         codes, 2 * dec_slots * count // LANES, LANES // 2)

        drain(ins[l], recv_sem.at[l])
        far = ins[l][...].astype(F32).reshape(count * halo_slots, width).astype(BF)
        table[own:table_rows, :] = (0.5 * dot(far, ef[l, width : 2 * width, :])).astype(BF)
        total[...] = jnp.zeros_like(total)

        @pl.loop(0, slots // EDGE_ROWS)
        def _(step):
            rows = rows_of(step, EDGE_ROWS)
            hidden = silu(early[rows, :] + dot(pick[rows, :], table[...]))
            result = normalize(dot(hidden, es[l]))
            total[...] += dot(pick_t[:, rows], result.astype(BF))
            if l < layers - 1:
                edges[rows, :] = (edges[rows, :].astype(F32) + result).astype(BF)

        hidden = silu(
            early_grid[0:own, :] + 0.5 * dot(total[...].astype(BF), nf[l, width:, :])
        )
        result = normalize(dot(hidden, ns[l]))
        nodes[...] = (nodes[...].astype(F32) + result).astype(BF)
        if l < layers - 1:
            halo_send(outs[l + 1], ins[l + 1], l + 1)

    half = width // 2
    chosen = dot(lists_pick(index_d[...], 2 * dec_slots), nodes[...])
    place = lax.broadcasted_iota(jnp.int32, (2 * dec_slots * count, half), 0)
    upper = (place % (2 * dec_slots)) >= dec_slots
    chosen = jnp.where(upper, chosen[:, half:], chosen[:, :half])
    out2[...] = chosen.reshape(count, 2 * dec_slots, half).astype(BF)
    post(out2, in2, layers)
    mesh_copy = pltpu.make_async_copy(nodes, mesh_o, done_sem.at[0])
    mesh_copy.start()

    l_df.wait()
    l_grid.wait()
    l_dedges.wait()
    steps = cells // ROWS

    @pl.loop(0, steps)
    def _(step):
        rows = rows_of(step)
        here = grid[rows, :]
        shared = 0.5 * dot(here, df[2 * width :, :])
        for b in range(branches):
            span = pl.ds(pl.multiple_of(b * cells + step * ROWS, ROWS), ROWS)
            early[span, :] = shared + 0.5 * dot(dedges[span, :], df[0:width, :])
        early_grid[rows, :] = 0.5 * dot(here, gf[0:width, :])

    drain(in2, recv_sem.at[layers])
    far = in2[...].astype(F32).reshape(count * 2 * dec_slots, half).astype(BF)
    place = lax.broadcasted_iota(jnp.int32, (2 * dec_slots * count, width), 0)
    upper = (place % (2 * dec_slots)) >= dec_slots
    chosen = jnp.where(
        upper, dot(far, df[width + half : 2 * width, :]), dot(far, df[width : width + half, :])
    )
    dtable[...] = (0.5 * chosen).astype(BF)

    @pl.loop(0, steps)
    def _(step):
        rows = rows_of(step)
        summed = None
        for b in range(branches):
            span = pl.ds(pl.multiple_of(b * cells + step * ROWS, ROWS), ROWS)
            hidden = silu(early[span, :] + dot(dpick[span, :], dtable[...]))
            result = normalize(dot(hidden, ds[...])).astype(BF).astype(F32)
            summed = result if summed is None else summed + result
        hidden = silu(early_grid[rows, :] + dot(summed.astype(BF), gf[width:, :]))
        result = normalize(dot(hidden, gs[...]))
        grid[rows, :] = (grid[rows, :].astype(F32) + result).astype(BF)
        pltpu.make_async_copy(grid.at[rows], grid_o.at[rows], done_sem.at[1 + step]).start()

    for b, buffer in enumerate([out0, out1, out2]):
        drain(buffer, send_sem.at[b])
    mesh_copy.wait()

    @pl.loop(0, steps)
    def _(step):
        rows = rows_of(step)
        pltpu.make_async_copy(grid.at[rows], grid_o.at[rows], done_sem.at[1 + step]).wait()


def shards(
    dims,
    mesh_nodes, mesh_edges, grid_state, decoder_edges, edge_send, edge_recv, halo_lists,
    decoder_lists, decoder_sources, edge_first, edge_second, node_first, node_second,
    decoder_first, decoder_second, grid_first, grid_second,
):
    own, width = mesh_nodes.shape
    slots = mesh_edges.shape[0]
    tile_lat, tile_lon = grid_state.shape[0], grid_state.shape[1]
    cells = tile_lat * tile_lon
    branches = decoder_edges.shape[0]
    count, halo_slots = halo_lists.shape[1], halo_lists.shape[2]
    dec_slots = decoder_lists.shape[2]
    layers = edge_first.shape[0]
    table_rows = own + count * halo_slots
    index_rows = -(-(2 * slots // LANES + branches * tile_lat) // LANES) * LANES
    hbm = pl.BlockSpec(memory_space=pl.ANY)
    vmem = pl.BlockSpec(memory_space=pltpu.VMEM)

    big = [mesh_nodes, mesh_edges, grid_state.reshape(cells, width),
           decoder_edges.reshape(branches * cells, width)]
    weights = [edge_first, edge_second, node_first, node_second,
               decoder_first, decoder_second, grid_first, grid_second]
    small = [edge_send.reshape(-1, LANES), edge_recv.reshape(-1, LANES), halo_lists[0].T,
             decoder_lists[0].T, decoder_sources]

    held = [pltpu.VMEM(a.shape, a.dtype) for a in big + weights]
    scratch = held + [
        pltpu.VMEM((index_rows, LANES), jnp.int32),
        pltpu.VMEM((2 * dec_slots, count), jnp.int32),
        pltpu.VMEM((slots, table_rows + own), BF),
        pltpu.VMEM((own, slots), BF),
        pltpu.VMEM((branches * cells, 2 * dec_slots * count), BF),
        pltpu.VMEM((table_rows + own, width), BF),
        pltpu.VMEM((2 * dec_slots * count, width), BF),
        pltpu.VMEM((max(slots, branches * cells), width), F32),
        pltpu.VMEM((max(cells, own), width), F32),
        pltpu.VMEM((own, width), F32),
        pltpu.VMEM((count, halo_slots, width), BF),
        pltpu.VMEM((count, halo_slots, width), BF),
        pltpu.VMEM((count, 2 * dec_slots, width // 2), BF),
        pltpu.VMEM((count, halo_slots, width), BF),
        pltpu.VMEM((count, halo_slots, width), BF),
        pltpu.VMEM((count, 2 * dec_slots, width // 2), BF),
        pltpu.SemaphoreType.DMA((8 + 4 * layers,)),
        pltpu.SemaphoreType.DMA((layers + 1,)),
        pltpu.SemaphoreType.DMA((layers + 1,)),
        pltpu.SemaphoreType.DMA((1 + cells // ROWS,)),
    ]
    mesh_final, grid_final = pl.pallas_call(
        functools.partial(kernel, dims),
        out_shape=(
            jax.ShapeDtypeStruct((own, width), BF),
            jax.ShapeDtypeStruct((cells, width), BF),
        ),
        in_specs=[hbm] * len(big) + [vmem] * len(small) + [hbm] * len(weights),
        out_specs=(hbm, hbm),
        scratch_shapes=scratch,
        compiler_params=pltpu.CompilerParams(
            collective_id=0, has_side_effects=True, vmem_limit_bytes=60 * 1024 * 1024
        ),
        name="processor",
    )(*big, *small, *weights)
    return mesh_final, grid_final.reshape(tile_lat, tile_lon, width)


def solution(mesh):
    both = ("lat", "lon")
    placed = (
        P(both, None),
        P(both, None),
        P("lat", "lon", None),
        P(None, "lat", "lon", None),
        P(both),
        P(both),
        P(both, None, None),
        P(both, None, None),
        P(None, "lat", "lon"),
    ) + (P(),) * 8
    dims = (mesh.shape["lat"], mesh.shape["lon"])
    return jax.shard_map(
        functools.partial(shards, dims),
        mesh=mesh,
        in_specs=placed,
        out_specs=(P(both, None), P("lat", "lon", None)),
        check_vma=False,
    )
```
